32 devices in a mesh: grp: 2 (over core), kv: 2 (over x), srv: 8 (over z, y).
Axes of the slice: x: 2, y: 2, z: 4, core: 2. Of those that a mesh axis runs over, the one named last changes fastest.
Arguments:
- queries: bfloat16 [2048, 8, 1024], P('srv', 'kv', 'grp'), may hold values from -120 to 120
- keys: bfloat16 [2048, 8, 128], P('srv', 'kv'), may hold values from -5 to 5
- values: bfloat16 [2048, 8, 128], P('srv', 'kv'), may hold values from -6 to 6
- lengths: int32 [4], replicated, may hold values from 1 to 1024, 2048 in all
- output_projection_weight: bfloat16 [8, 1024, 8192], P('kv', 'grp', 'srv'), may hold values from -0.0625 to 0.0625
Outputs:
- projected: bfloat16 [2048, 8192], P('srv', ('grp', 'kv'))
The draws below stay inside these ranges and needn't reach their ends.
Inputs may be any that keep to these rules, and one draw needn't show every extreme that they name: The 4 lengths sum to 2048; the longest document has exactly 1024 tokens.
All inputs are finite; a program needn't handle non-finite values.
Results may differ from the reference program's by a relative error of at most 0.017.
Values may be sent and summed in bfloat16 or wider, within the bound.
A program may use at most 128 MiB of HBM per device.

```python
import math
import jax
import jax.numpy as jnp
import numpy as np
from jax import lax

MODEL_WIDTH = 8192
QUERY_HEADS = 64
KEY_VALUE_HEADS = 8
HEAD_WIDTH = 128
TOK_DEV = 256
QUERY_PER_KEY = 8
PACK_TOKENS = 2048
MOST = 1024
DOCS = 4
N_GRP = 2
N_KV = 2
N_SRV = 8


def shared_draw(key):
    base = jax.random.fold_in(key, 1234)
    key_random_seed, query_random_seed = jax.random.split(base, 2)
    key_tensor = jnp.clip(jax.random.normal(key_random_seed, (PACK_TOKENS, KEY_VALUE_HEADS, HEAD_WIDTH), jnp.float32), -5.0, 5.0)
    query_tensor = jnp.clip(jax.random.normal(query_random_seed, (PACK_TOKENS, KEY_VALUE_HEADS, QUERY_PER_KEY * HEAD_WIDTH), jnp.float32), -5.0, 5.0)
    return (query_tensor, key_tensor)


def draw_queries(key, part):
    return shared_draw(key)[0].astype(jnp.bfloat16)


def draw_keys(key, part):
    return shared_draw(key)[1].astype(jnp.bfloat16)


def levels(key, dims, shards, least, high):
    def one(dim, parts):
        heights = jax.random.uniform(jax.random.fold_in(jax.random.fold_in(key, 6), dim), (parts,), jnp.float32, least / len(shards), high / len(shards))
        return jnp.repeat(jnp.exp(heights), dims[dim] // parts).reshape((-1,) + (1,) * (len(dims) - dim - 1))

    factor_of = one(*shards[0])
    for cut in shards[1:]:
        factor_of = factor_of * one(*cut)
    return factor_of


def length_profile(count, total, reach, skew):
    portions = [(1 << 20) // math.isqrt(standing ** skew) + 1 for standing in range(2, count + 1)]
    surplus, given = total - reach - (count - 1), [1] * (count - 1)
    while surplus > 0:
        candidates = [i for i in range(count - 1) if given[i] < reach]
        whole, budget = sum([portions[i] for i in candidates]), surplus
        for i in candidates:
            more = min(reach - given[i], max(1, budget * portions[i] // whole), surplus)
            given[i] = given[i] + more
            surplus = surplus - more
    return np.array([reach] + given)


def uneven_parts(own_key, amount, total, most, slope):
    if amount == 2:
        one = jax.random.randint(own_key, (), max(1, total - most), min(most, total - 1) + 1)
        return jnp.stack([one, total - one])
    tallies = jnp.asarray(length_profile(amount, total, most, slope), jnp.int32)
    couples = (amount - 1) // 2
    giver, receiver = tallies[1:1 + 2 * couples:2], tallies[2:2 + 2 * couples:2]
    margin = jnp.minimum(giver - 1, most - receiver)
    shifted = jax.random.randint(jax.random.fold_in(own_key, 1), (couples,), 0, 1 << 20) % (margin + 1)
    tallies = tallies.at[1:1 + 2 * couples:2].set(giver - shifted).at[2:2 + 2 * couples:2].set(receiver + shifted)
    return tallies[jax.random.permutation(jax.random.fold_in(own_key, 2), amount)]


def normal_values(rng, shape, deviation, bound, cuts=(), held_as=jnp.bfloat16):
    result = deviation * jax.random.normal(rng, shape, jnp.float32)
    if cuts:
        result = result * levels(rng, shape, cuts, -0.22, 0.18)
    return jnp.clip(result, -bound, bound).astype(held_as)


def setup_inputs(seed: int = 0) -> dict:
    key_list = jax.random.split(jax.random.key(seed), 6)
    return {
        "queries": draw_queries(jax.random.fold_in(key_list[5], 71), 0),
        "keys": draw_keys(jax.random.fold_in(key_list[5], 71), 0),
        "values": normal_values(key_list[2], (PACK_TOKENS, KEY_VALUE_HEADS, HEAD_WIDTH), 1.0, 6.0, ((0, 8), (1, 2))),
        "lengths": uneven_parts(key_list[3], DOCS, PACK_TOKENS, MOST, 2).astype(jnp.int32),
        "output_projection_weight": normal_values(key_list[4], (KEY_VALUE_HEADS, QUERY_PER_KEY * HEAD_WIDTH, MODEL_WIDTH), (QUERY_HEADS * HEAD_WIDTH) ** -0.5, 0.0625, ((0, 2), (1, 2), (2, 8))),
    }


def doc_starts(lengths, position):
    starts = jnp.cumsum(lengths) - lengths
    chosen = jnp.where(starts[None, :] <= position[:, None], starts[None, :], 0)
    return lax.optimization_barrier(jnp.max(chosen, axis=1))

def attend_exact(query_block_rows, window_keys, window_values, query_pos, key_pos, lengths):
    token_count = query_block_rows.shape[0]
    split_output = query_block_rows.astype(jnp.float32).reshape(token_count, KEY_VALUE_HEADS, QUERY_PER_KEY, HEAD_WIDTH)
    scores = jnp.einsum('tjhd,wjd->jhtw', split_output, window_keys.astype(jnp.float32)) * (1.0 / math.sqrt(HEAD_WIDTH))
    first_key = doc_starts(lengths, query_pos)
    allowed = (key_pos[None, :] >= first_key[:, None]) & (key_pos[None, :] <= query_pos[:, None])
    scores = jnp.where(allowed[None, None], scores, -jnp.inf)
    peak = lax.optimization_barrier(jnp.max(scores, axis=3, keepdims=True))
    weights = jnp.exp(scores - peak)
    total = lax.optimization_barrier(jnp.sum(weights, axis=3))
    rounded = lax.optimization_barrier(weights.astype(jnp.bfloat16))
    numer = jnp.einsum('jhtw,wjd->tjhd', rounded.astype(jnp.float32), window_values.astype(jnp.float32))
    final_output = numer / jnp.transpose(total, (2, 0, 1))[..., None]
    return final_output.astype(jnp.bfloat16).reshape(token_count, KEY_VALUE_HEADS, QUERY_PER_KEY * HEAD_WIDTH)

def reference(queries, keys, values, lengths, output_projection_weight):
    window = MOST + TOK_DEV
    keys_padded = jnp.pad(keys, ((MOST, 0), (0, 0), (0, 0)))
    values_padded = jnp.pad(values, ((MOST, 0), (0, 0), (0, 0)))

    def one_block(index):
        start = index * TOK_DEV
        query_block_rows = lax.dynamic_slice_in_dim(queries, start, TOK_DEV, 0)
        window_keys = lax.dynamic_slice_in_dim(keys_padded, start, window, 0)
        window_values = lax.dynamic_slice_in_dim(values_padded, start, window, 0)
        query_pos = start + jnp.arange(TOK_DEV, dtype=jnp.int32)
        key_pos = start - MOST + jnp.arange(window, dtype=jnp.int32)
        return attend_exact(query_block_rows, window_keys, window_values, query_pos, key_pos, lengths)
    block_list = lax.map(one_block, jnp.arange(N_SRV, dtype=jnp.int32))
    attention_output = block_list.reshape(PACK_TOKENS, KEY_VALUE_HEADS, QUERY_PER_KEY * HEAD_WIDTH)
    heads_per_group = KEY_VALUE_HEADS // N_KV
    half_width = QUERY_PER_KEY * HEAD_WIDTH // N_GRP
    attended_split = attention_output.reshape(PACK_TOKENS, N_KV, heads_per_group, N_GRP, half_width)
    weight_split = output_projection_weight.reshape(N_KV, heads_per_group, N_GRP, half_width, MODEL_WIDTH)
    summed = jnp.zeros((PACK_TOKENS, MODEL_WIDTH), jnp.float32)
    for half_index in range(N_GRP):
        for group_index in range(N_KV):
            left = attended_split[:, group_index, :, half_index, :].reshape(PACK_TOKENS, heads_per_group * half_width)
            right = weight_split[group_index, :, half_index].reshape(heads_per_group * half_width, MODEL_WIDTH)
            partial_sum = jnp.dot(left, right, preferred_element_type=jnp.float32).astype(jnp.bfloat16)
            partial_sum = lax.optimization_barrier(partial_sum)
            summed = summed + partial_sum.astype(jnp.float32)
    return summed.astype(jnp.bfloat16)
```

```python
import math

import jax
import jax.numpy as jnp
from jax import lax
from jax.sharding import PartitionSpec as P

REACH = 4


def from_behind(block, axis, distance):
    devices = range(lax.axis_size(axis))
    route = [(i - distance, i) for i in devices if i - distance in devices]
    return lax.ppermute(block, axis, route)


def doc_starts(lengths, position):
    starts = jnp.cumsum(lengths) - lengths
    chosen = jnp.where(starts[None, :] <= position[:, None], starts[None, :], 0)
    return jnp.max(chosen, axis=1)


def attend(queries, window_keys, window_values, query_pos, key_pos, lengths):
    token_count = queries.shape[0]
    groups = queries.shape[1]
    head_size = window_keys.shape[2]
    heads = queries.shape[2] // head_size
    split_output = queries.reshape(token_count, groups, heads, head_size)
    scores = jnp.einsum(
        "tjhd,wjd->jhtw", split_output, window_keys, preferred_element_type=jnp.float32
    )
    scores = scores * (1.0 / math.sqrt(head_size))
    first_key = doc_starts(lengths, query_pos)
    allowed = (key_pos[None, :] >= first_key[:, None]) & (key_pos[None, :] <= query_pos[:, None])
    scores = jnp.where(allowed[None, None], scores, -jnp.inf)
    peak = jnp.max(scores, axis=3, keepdims=True)
    weights = jnp.exp(scores - peak)
    total = jnp.sum(weights, axis=3)
    numer = jnp.einsum(
        "jhtw,wjd->tjhd",
        weights.astype(jnp.bfloat16),
        window_values,
        preferred_element_type=jnp.float32,
    )
    final_output = numer / jnp.transpose(total, (2, 0, 1))[..., None]
    return final_output.astype(jnp.bfloat16).reshape(token_count, groups * heads * head_size)


def on_device(queries, keys, values, lengths, output_projection_weight):
    token_count = queries.shape[0]
    shard = lax.axis_index("srv")
    stacked = jnp.stack([keys, values])
    arrived = [stacked]
    for distance in range(1, REACH + 1):
        arrived.append(from_behind(stacked, "srv", distance))
    window = jnp.concatenate(arrived[::-1], axis=1)
    query_pos = shard * token_count + jnp.arange(token_count, dtype=jnp.int32)
    key_pos = (shard - REACH) * token_count + jnp.arange(window.shape[1], dtype=jnp.int32)
    attention_output = attend(queries, window[0], window[1], query_pos, key_pos, lengths)
    inner = attention_output.shape[1]
    weight = output_projection_weight.reshape(inner, output_projection_weight.shape[2])
    everyone = lax.all_gather(attention_output, "srv", axis=0, tiled=True)
    partial_sum = jnp.dot(everyone, weight, preferred_element_type=jnp.float32)
    summed = lax.psum_scatter(
        partial_sum.astype(jnp.bfloat16), ("grp", "kv"), scatter_dimension=0, tiled=True
    )
    return to_token_owners(summed, token_count)


def to_token_owners(summed, token_count):
    shards = lax.axis_size("srv")
    blocks = lax.axis_size("grp") * lax.axis_size("kv")
    per = shards // blocks
    width = summed.shape[1]
    mine = lax.axis_index("srv") % per
    out = jnp.zeros((token_count, per * width), summed.dtype)
    for shift in range(per):
        route = []
        for block in range(blocks):
            for shard in range(shards):
                to = block * per + (shard % per + shift) % per
                route.append((block * shards + shard, (shard // per) * shards + to))
        leaving = lax.dynamic_slice_in_dim(
            summed, ((mine + shift) % per) * token_count, token_count, 0
        )
        came = lax.ppermute(leaving, ("grp", "kv", "srv"), route)
        out = lax.dynamic_update_slice_in_dim(out, came, ((mine - shift) % per) * width, 1)
    return out


def solution(mesh):
    placed = (
        P("srv", "kv", "grp"),
        P("srv", "kv", None),
        P("srv", "kv", None),
        P(),
        P("kv", "grp", "srv"),
    )
    return jax.shard_map(
        on_device, mesh=mesh, in_specs=placed, out_specs=P("srv", ("grp", "kv")), check_vma=False
    )
```

```python
import functools
import math

import jax
import jax.numpy as jnp
from jax import lax
from jax.experimental import pallas as pl
from jax.experimental.pallas import tpu as pltpu
from jax.sharding import PartitionSpec as P

REACH = 4
PIECES = 4
FAR = -1e30
MESH = pl.DeviceIdType.MESH


def layer(plan, lengths, q_ref, kv_ref, w_ref, out_ref, kvw, bias, abuf, wbuf, send1, recv1,
          acc, send2, recv2, send3, kv_s, kv_r, y_s, y_r, swap_s, swap_r, own_w, w_s, w_r,
          a_s, a_r, s1, r1, s2, r2, s3, r3):
    head, halves, lanes, pairs, chunk, own_chunks = plan
    tokens, inner = q_ref.shape
    groups = kvw.shape[3] // head
    heads = inner // (groups * head)
    span = heads * head
    chunks = wbuf.shape[0]
    columns = w_ref.shape[1]
    rows = halves * tokens
    a, g, s = lax.axis_index("grp"), lax.axis_index("kv"), lax.axis_index("srv")
    u, v = s // pairs, s % pairs
    q = a * halves + g

    core = (1 - a, g, s)
    beside = (a, g, u * pairs + 1 - v)
    ahead = (a, g, s + pairs)
    behind = (a, g, s - pairs)
    across = (u // halves, u % halves, q * pairs + v)
    away = q != u
    right, left = u + 1 < lanes, u > 0

    def other_half(k):
        return (a, (g + k) % halves, s)

    barrier = pltpu.get_barrier_semaphore()

    def greet(device):
        pl.semaphore_signal(barrier, inc=1, device_id=device, device_id_type=MESH)

    greet(core)
    greet(beside)
    for k in range(1, halves):
        greet(other_half(k))
    pl.when(right)(lambda: greet(ahead))
    pl.when(left)(lambda: greet(behind))
    pl.when(away)(lambda: greet(across))
    peers = jnp.int32(1 + halves)
    for there in (right, left, away):
        peers = peers + jnp.where(there, 1, 0)
    pl.semaphore_wait(barrier, peers)

    def remote(src, dst, send, recv, device):
        return pltpu.make_async_remote_copy(
            src_ref=src, dst_ref=dst, send_sem=send, recv_sem=recv,
            device_id=device, device_id_type=MESH,
        )

    def hop(d):
        src = kv_ref.at[a] if d == 2 else kvw.at[a, 2]
        return remote(src, kvw.at[a, d], kv_s.at[d // 2 - 1], kv_r.at[d // 2 - 1], ahead)

    def sideways(d):
        src = kv_ref.at[a] if d == 0 else kvw.at[a, d]
        slot = jnp.where(v == 0, d + 1, d - 1)
        return remote(src, kvw.at[a, slot], y_s.at[d // 2], y_r.at[slot // 2], beside)

    def came(d):
        return remote(kv_ref.at[a], kvw.at[a, d], y_s.at[0], y_r.at[d // 2], beside)

    def swap(d):
        return remote(kvw.at[a, d], kvw.at[a, d], swap_s.at[d - 1], swap_r.at[d - 1], core)

    def swapped(d):
        return remote(kvw.at[a, d], kvw.at[1 - a, d], swap_s.at[d - 1], swap_r.at[d - 1], core)

    depth = inner // PIECES

    def weight(c, p):
        part = pl.ds(p * depth, depth)
        return remote(
            w_ref.at[part, pl.ds(c * chunk, chunk)], wbuf.at[own_chunks + c, part],
            w_s.at[c, p], w_r.at[c, p], beside,
        )

    def own_weight(c):
        return pltpu.make_async_copy(
            w_ref.at[:, pl.ds(c * chunk, chunk)], wbuf.at[c], own_w.at[c]
        )

    two, four = u >= 1, u >= 2
    pl.when(right)(lambda: hop(2).start())
    pl.when(v == 0)(lambda: sideways(0).start())
    weight(0, 0).start()
    for c in range(own_chunks):
        own_weight(c).start()
    kvw[0, 0] = kv_ref[0]
    kvw[1, 0] = kv_ref[1]
    for d in range(1, REACH + 1):
        @pl.when(s < d)
        def _():
            kvw[0, d] = jnp.zeros(kvw.shape[2:], kvw.dtype)
            kvw[1, d] = jnp.zeros(kvw.shape[2:], kvw.dtype)

    row = lax.broadcasted_iota(jnp.int32, (tokens, 1), 0)
    query_pos = s * tokens + row
    first = jnp.zeros((tokens, 1), jnp.int32)
    start = jnp.int32(0)
    for i in range(lengths.shape[0]):
        first = jnp.where(query_pos >= start, start, first)
        start = start + lengths[i]
    lane = lax.broadcasted_iota(jnp.int32, (tokens, tokens), 1)
    for d in range(REACH + 1):
        key_pos = (s - d) * tokens + lane
        allowed = (key_pos >= first) & (key_pos <= query_pos)
        bias[:, d * tokens:(d + 1) * tokens] = jnp.where(allowed, 0.0, FAR)

    @pl.when(two)
    def _():
        hop(2).wait_recv()
        pl.when(right)(lambda: hop(4).start())
        sideways(2).start()
        swap(2).start()

    weight(0, 1).start()

    @pl.when(s >= 1)
    def _():
        came(1).wait_recv()
        swap(1).start()

    @pl.when(four)
    def _():
        hop(4).wait_recv()
        pl.when(v == 1)(lambda: sideways(4).start())
        swap(4).start()

    for p in range(2, PIECES):
        weight(0, p).start()
    for c in range(1, own_chunks):
        for p in range(PIECES):
            weight(c, p).start()

    @pl.when(s >= 3)
    def _():
        came(3).wait_recv()
        swap(3).start()

    for d in range(1, REACH + 1):
        pl.when(s >= d)(lambda d=d: swapped(d).wait_recv())

    def relay(way, d, j):
        block = u - (d - 1) if way == 0 else u + (d - 1)
        part = abuf.at[block, :, pl.ds(pl.multiple_of(j * span, span), span)]
        return remote(part, part, a_s.at[way, d - 1, j], a_r.at[way, d - 1, j],
                      ahead if way == 0 else behind)

    def relayed(way, d, j):
        block = u - d if way == 0 else u + d
        part = abuf.at[block, :, pl.ds(pl.multiple_of(j * span, span), span)]
        return remote(part, part, a_s.at[way, d - 1, j], a_r.at[way, d - 1, j],
                      behind if way == 0 else ahead)

    def holds(way, d):
        return u >= d if way == 0 else u + d < lanes

    def may_send(way):
        return right if way == 0 else left

    def forward(d, j):
        for way in range(2):
            @pl.when(holds(way, d - 1))
            def _():
                relayed(way, d - 1, j).wait_recv()
                pl.when(may_send(way))(lambda: relay(way, d, j).start())

    factor = math.log2(math.e) / math.sqrt(head)

    def per_group(j, carry):
        at = pl.ds(pl.multiple_of(j * head, head), head)

        def per_head(h, inside):
            mine = pl.ds(pl.multiple_of(j * span + h * head, head), head)
            window = kvw[0, :, :, at].reshape((REACH + 1) * tokens, head)
            scores = lax.dot_general(
                q_ref[:, mine], window, (((1,), (1,)), ((), ())),
                preferred_element_type=jnp.float32,
            ) + bias[...]
            peak = jnp.max(scores, axis=1, keepdims=True)
            weights = jnp.exp2((scores - peak) * factor)
            total = jnp.sum(weights, axis=1, keepdims=True)
            numer = jnp.dot(
                weights.astype(jnp.bfloat16),
                kvw[1, :, :, at].reshape((REACH + 1) * tokens, head),
                preferred_element_type=jnp.float32,
            )
            abuf[u, :, mine] = (numer / total).astype(abuf.dtype)
            return inside

        lax.fori_loop(0, heads, per_head, 0)
        for way in range(2):
            pl.when(may_send(way))(lambda: relay(way, 1, j).start())
        pl.when(j >= 2)(lambda: forward(2, j - 2))
        return carry

    lax.fori_loop(0, groups, per_group, 0)

    def over_groups(low, body):
        def step(j, carry):
            body(j)
            return carry

        lax.fori_loop(low, groups, step, 0)

    over_groups(max(0, groups - 2), lambda j: forward(2, j))
    for d in range(3, lanes):
        over_groups(0, lambda j: forward(d, j))

    def last(j):
        for way in range(2):
            pl.when(holds(way, lanes - 1))(lambda: relayed(way, lanes - 1, j).wait_recv())

    over_groups(0, last)

    def to_core(c):
        return remote(send1.at[c], recv1.at[c], s1.at[c], r1.at[c], core)

    def to_half(c, k):
        return remote(send2.at[c, pl.ds((g + k) % halves * tokens, tokens)], recv2.at[c, k - 1],
                      s2.at[c, k - 1], r2.at[c, k - 1], other_half(k))

    def result(c):
        own = c < own_chunks
        offset = jnp.where(own, v * columns + c * chunk,
                           (1 - v) * columns + (c - own_chunks) * chunk)
        return out_ref.at[:, pl.ds(pl.multiple_of(offset, chunk), chunk)]

    def to_owner(c):
        return remote(send3.at[c], result(c), s3.at[c], r3.at[c], across)

    def to_self(c):
        return pltpu.make_async_copy(send3.at[c], result(c), r3.at[c])

    def product(half, c):
        left_side = abuf[pl.ds(half * halves, halves)].reshape(rows, inner)
        return jnp.dot(left_side, wbuf[c], preferred_element_type=jnp.float32)

    def second(c):
        for k in range(1, halves):
            to_half(c, k).wait_recv()
        total = acc[c, pl.ds(g * tokens, tokens)]
        for k in range(1, halves):
            total = total + recv2[c, k - 1].astype(jnp.float32)
        send3[c] = total.astype(send3.dtype)
        pl.when(away)(lambda: to_owner(c).start())
        pl.when(jnp.logical_not(away))(lambda: to_self(c).start())

    def per_chunk(c, carry):
        pl.when(c < own_chunks)(lambda: own_weight(c).wait())

        @pl.when(c >= own_chunks)
        def _():
            for p in range(PIECES):
                weight(c - own_chunks, p).wait_recv()

        send1[c] = product(1 - a, c).astype(send1.dtype)
        to_core(c).start()
        acc[c] = product(a, c)
        pl.when(c >= 1)(lambda: second(c - 1))
        to_core(c).wait_recv()
        total = acc[c] + recv1[c].astype(jnp.float32)
        acc[c] = total
        send2[c] = total.astype(send2.dtype)
        for k in range(1, halves):
            to_half(c, k).start()
        return carry

    lax.fori_loop(0, chunks, per_chunk, 0)
    second(chunks - 1)

    pl.when(right)(lambda: hop(2).wait_send())
    pl.when(two & right)(lambda: hop(4).wait_send())
    pl.when(v == 0)(lambda: sideways(0).wait_send())
    pl.when(two)(lambda: sideways(2).wait_send())
    pl.when(four & (v == 1))(lambda: sideways(4).wait_send())
    for d in range(1, REACH + 1):
        pl.when(s >= d)(lambda d=d: swap(d).wait_send())
    for c in range(own_chunks):
        for p in range(PIECES):
            weight(c, p).wait_send()
    for d in range(1, lanes):
        for way in range(2):
            @pl.when(holds(way, d - 1) & may_send(way))
            def _():
                over_groups(0, lambda j: relay(way, d, j).wait_send())

    def finish(c, carry):
        to_core(c).wait_send()
        for k in range(1, halves):
            to_half(c, k).wait_send()

        @pl.when(away)
        def _():
            to_owner(c).wait_send()
            to_owner(c).wait_recv()

        pl.when(jnp.logical_not(away))(lambda: to_self(c).wait())
        return carry

    lax.fori_loop(0, chunks, finish, 0)


def on_device(queries, keys, values, lengths, output_projection_weight):
    tokens = queries.shape[0]
    cores, halves = lax.axis_size("grp"), lax.axis_size("kv")
    lanes = cores * halves
    pairs = lax.axis_size("srv") // lanes
    assert cores == 2 and pairs == 2
    q = queries.reshape(tokens, -1)
    inner = q.shape[1]
    kv = jnp.stack([keys.reshape(tokens, -1), values.reshape(tokens, -1)])
    weight = output_projection_weight.reshape(inner, -1)
    columns = weight.shape[1]
    chunk = max(128, columns // 4)
    own_chunks = columns // chunk
    chunks = own_chunks * pairs
    groups, head = keys.shape[1], keys.shape[2]
    rows = halves * tokens
    dma = pltpu.SemaphoreType.DMA
    bf16, f32 = jnp.bfloat16, jnp.float32
    vmem = pl.BlockSpec(memory_space=pltpu.VMEM)
    return pl.pallas_call(
        functools.partial(layer, (head, halves, lanes, pairs, chunk, own_chunks)),
        out_shape=jax.ShapeDtypeStruct((tokens, pairs * columns), bf16),
        in_specs=[
            pl.BlockSpec(memory_space=pltpu.SMEM), vmem, vmem,
            pl.BlockSpec(memory_space=pl.ANY),
        ],
        out_specs=pl.BlockSpec(memory_space=pl.ANY),
        scratch_shapes=[
            pltpu.VMEM((2, REACH + 1, tokens, kv.shape[2]), bf16),
            pltpu.VMEM((tokens, (REACH + 1) * tokens), f32),
            pltpu.VMEM((lanes, tokens, inner), bf16),
            pltpu.VMEM((chunks, inner, chunk), bf16),
            pltpu.VMEM((chunks, rows, chunk), bf16),
            pltpu.VMEM((chunks, rows, chunk), bf16),
            pltpu.VMEM((chunks, rows, chunk), f32),
            pltpu.VMEM((chunks, rows, chunk), bf16),
            pltpu.VMEM((chunks, halves - 1, tokens, chunk), bf16),
            pltpu.VMEM((chunks, tokens, chunk), bf16),
            dma((2,)), dma((2,)), dma((3,)), dma((2,)), dma((REACH,)), dma((REACH,)),
            dma((own_chunks,)), dma((own_chunks, PIECES)), dma((own_chunks, PIECES)),
            dma((2, lanes - 1, groups)), dma((2, lanes - 1, groups)),
            dma((chunks,)), dma((chunks,)),
            dma((chunks, halves - 1)), dma((chunks, halves - 1)),
            dma((chunks,)), dma((chunks,)),
        ],
        compiler_params=pltpu.CompilerParams(
            collective_id=0, has_side_effects=True, vmem_limit_bytes=60 * 1024 * 1024
        ),
    )(lengths, q, kv, weight)


def solution(mesh):
    placed = (
        P("srv", "kv", "grp"),
        P("srv", "kv", None),
        P("srv", "kv", None),
        P(),
        P("kv", "grp", "srv"),
    )
    return jax.shard_map(
        on_device, mesh=mesh, in_specs=placed, out_specs=P("srv", ("grp", "kv")), check_vma=False
    )
```

```python
import functools
import math

import jax
import jax.numpy as jnp
from jax import lax
from jax.experimental import pallas as pl
from jax.experimental.pallas import tpu as pltpu
from jax.sharding import PartitionSpec as P

REACH = 4
PIECES = 4
FAR = -1e30
MESH = pl.DeviceIdType.MESH


def layer(plan, lengths, q_ref, kv_ref, w_ref, out_ref, kvw, bias, abuf, wbuf, send1, recv1,
          acc, send2, recv2, send3, kv_s, kv_r, y_s, y_r, swap_s, swap_r, own_w, w_s, w_r,
          a_s, a_r, s1, r1, s2, r2, s3, r3):
    head, halves, lanes, pairs, chunk, own_chunks = plan
    tokens, inner = q_ref.shape
    groups = kvw.shape[3] // head
    heads = inner // (groups * head)
    span = heads * head
    chunks = wbuf.shape[0]
    columns = w_ref.shape[1]
    rows = halves * tokens
    a, g, s = lax.axis_index("grp"), lax.axis_index("kv"), lax.axis_index("srv")
    u, v = s // pairs, s % pairs
    q = a * halves + g

    core = (1 - a, g, s)
    beside = (a, g, u * pairs + 1 - v)
    ahead = (a, g, s + pairs)
    behind = (a, g, s - pairs)
    across = (u // halves, u % halves, q * pairs + v)
    away = q != u
    right, left = u + 1 < lanes, u > 0

    def other_half(k):
        return (a, (g + k) % halves, s)

    barrier = pltpu.get_barrier_semaphore()

    def greet(device):
        pl.semaphore_signal(barrier, inc=1, device_id=device, device_id_type=MESH)

    greet(core)
    greet(beside)
    for k in range(1, halves):
        greet(other_half(k))
    pl.when(right)(lambda: greet(ahead))
    pl.when(left)(lambda: greet(behind))
    pl.when(away)(lambda: greet(across))
    peers = jnp.int32(1 + halves)
    for there in (right, left, away):
        peers = peers + jnp.where(there, 1, 0)
    pl.semaphore_wait(barrier, peers)

    def remote(src, dst, send, recv, device):
        return pltpu.make_async_remote_copy(
            src_ref=src, dst_ref=dst, send_sem=send, recv_sem=recv,
            device_id=device, device_id_type=MESH,
        )

    def hop(d):
        src = kv_ref.at[a] if d == 2 else kvw.at[a, 2]
        return remote(src, kvw.at[a, d], kv_s.at[d // 2 - 1], kv_r.at[d // 2 - 1], ahead)

    def sideways(d):
        src = kv_ref.at[a] if d == 0 else kvw.at[a, d]
        slot = jnp.where(v == 0, d + 1, d - 1)
        return remote(src, kvw.at[a, slot], y_s.at[d // 2], y_r.at[slot // 2], beside)

    def came(d):
        return remote(kv_ref.at[a], kvw.at[a, d], y_s.at[0], y_r.at[d // 2], beside)

    def swap(d):
        return remote(kvw.at[a, d], kvw.at[a, d], swap_s.at[d - 1], swap_r.at[d - 1], core)

    def swapped(d):
        return remote(kvw.at[a, d], kvw.at[1 - a, d], swap_s.at[d - 1], swap_r.at[d - 1], core)

    depth = inner // PIECES

    def weight(c, p):
        part = pl.ds(p * depth, depth)
        return remote(
            w_ref.at[part, pl.ds(c * chunk, chunk)], wbuf.at[own_chunks + c, part],
            w_s.at[c, p], w_r.at[c, p], beside,
        )

    def own_weight(c):
        return pltpu.make_async_copy(
            w_ref.at[:, pl.ds(c * chunk, chunk)], wbuf.at[c], own_w.at[c]
        )

    two, four = u >= 1, u >= 2
    pl.when(right)(lambda: hop(2).start())
    pl.when(v == 0)(lambda: sideways(0).start())
    weight(0, 0).start()
    for c in range(own_chunks):
        own_weight(c).start()
    kvw[0, 0] = kv_ref[0]
    kvw[1, 0] = kv_ref[1]
    for d in range(1, REACH + 1):
        @pl.when(s < d)
        def _():
            kvw[0, d] = jnp.zeros(kvw.shape[2:], kvw.dtype)
            kvw[1, d] = jnp.zeros(kvw.shape[2:], kvw.dtype)

    row = lax.broadcasted_iota(jnp.int32, (tokens, 1), 0)
    query_pos = s * tokens + row
    first = jnp.zeros((tokens, 1), jnp.int32)
    start = jnp.int32(0)
    for i in range(lengths.shape[0]):
        first = jnp.where(query_pos >= start, start, first)
        start = start + lengths[i]
    lane = lax.broadcasted_iota(jnp.int32, (tokens, tokens), 1)
    for d in range(REACH + 1):
        key_pos = (s - d) * tokens + lane
        allowed = (key_pos >= first) & (key_pos <= query_pos)
        bias[:, d * tokens:(d + 1) * tokens] = jnp.where(allowed, 0.0, FAR)

    @pl.when(two)
    def _():
        hop(2).wait_recv()
        pl.when(right)(lambda: hop(4).start())
        sideways(2).start()
        swap(2).start()

    weight(0, 1).start()

    @pl.when(s >= 1)
    def _():
        came(1).wait_recv()
        swap(1).start()

    @pl.when(four)
    def _():
        hop(4).wait_recv()
        pl.when(v == 1)(lambda: sideways(4).start())
        swap(4).start()

    for p in range(2, PIECES):
        weight(0, p).start()
    for c in range(1, own_chunks):
        for p in range(PIECES):
            weight(c, p).start()

    @pl.when(s >= 3)
    def _():
        came(3).wait_recv()
        swap(3).start()

    for d in range(1, REACH + 1):
        pl.when(s >= d)(lambda d=d: swapped(d).wait_recv())

    def relay(way, d, j):
        block = u - (d - 1) if way == 0 else u + (d - 1)
        part = abuf.at[block, :, pl.ds(pl.multiple_of(j * span, span), span)]
        return remote(part, part, a_s.at[way, d - 1, j], a_r.at[way, d - 1, j],
                      ahead if way == 0 else behind)

    def relayed(way, d, j):
        block = u - d if way == 0 else u + d
        part = abuf.at[block, :, pl.ds(pl.multiple_of(j * span, span), span)]
        return remote(part, part, a_s.at[way, d - 1, j], a_r.at[way, d - 1, j],
                      behind if way == 0 else ahead)

    def holds(way, d):
        return u >= d if way == 0 else u + d < lanes

    def may_send(way):
        return right if way == 0 else left

    def forward(d, j):
        for way in range(2):
            @pl.when(holds(way, d - 1))
            def _():
                relayed(way, d - 1, j).wait_recv()
                pl.when(may_send(way))(lambda: relay(way, d, j).start())

    factor = math.log2(math.e) / math.sqrt(head)

    def per_group(j, carry):
        at = pl.ds(pl.multiple_of(j * head, head), head)

        def per_head(h, inside):
            mine = pl.ds(pl.multiple_of(j * span + h * head, head), head)
            window = kvw[0, :, :, at].reshape((REACH + 1) * tokens, head)
            scores = lax.dot_general(
                q_ref[:, mine], window, (((1,), (1,)), ((), ())),
                preferred_element_type=jnp.float32,
            ) + bias[...]
            peak = jnp.max(scores, axis=1, keepdims=True)
            weights = jnp.exp2((scores - peak) * factor)
            total = jnp.sum(weights, axis=1, keepdims=True)
            numer = jnp.dot(
                weights.astype(jnp.bfloat16),
                kvw[1, :, :, at].reshape((REACH + 1) * tokens, head),
                preferred_element_type=jnp.float32,
            )
            abuf[u, :, mine] = (numer / total).astype(abuf.dtype)
            return inside

        lax.fori_loop(0, heads, per_head, 0)
        for way in range(2):
            pl.when(may_send(way))(lambda: relay(way, 1, j).start())
        pl.when(j >= 2)(lambda: forward(2, j - 2))
        return carry

    lax.fori_loop(0, groups, per_group, 0)

    def over_groups(low, body):
        def step(j, carry):
            body(j)
            return carry

        lax.fori_loop(low, groups, step, 0)

    over_groups(max(0, groups - 2), lambda j: forward(2, j))
    for d in range(3, lanes):
        over_groups(0, lambda j: forward(d, j))

    def last(j):
        for way in range(2):
            pl.when(holds(way, lanes - 1))(lambda: relayed(way, lanes - 1, j).wait_recv())

    over_groups(0, last)

    def to_core(c):
        return remote(send1.at[c], recv1.at[c], s1.at[c], r1.at[c], core)

    def to_half(c, k):
        return remote(send2.at[c, pl.ds((g + k) % halves * tokens, tokens)], recv2.at[c, k - 1],
                      s2.at[c, k - 1], r2.at[c, k - 1], other_half(k))

    def result(c):
        own = c < own_chunks
        offset = jnp.where(own, v * columns + c * chunk,
                           (1 - v) * columns + (c - own_chunks) * chunk)
        return out_ref.at[:, pl.ds(pl.multiple_of(offset, chunk), chunk)]

    def to_owner(c):
        return remote(send3.at[c], result(c), s3.at[c], r3.at[c], across)

    def to_self(c):
        return pltpu.make_async_copy(send3.at[c], result(c), r3.at[c])

    def product(half, c):
        left_side = abuf[pl.ds(half * halves, halves)].reshape(rows, inner)
        return jnp.dot(left_side, wbuf[c], preferred_element_type=jnp.float32)

    def second(c):
        for k in range(1, halves):
            to_half(c, k).wait_recv()
        total = acc[c, pl.ds(g * tokens, tokens)]
        for k in range(1, halves):
            total = total + recv2[c, k - 1].astype(jnp.float32)
        send3[c] = total.astype(send3.dtype)
        pl.when(away)(lambda: to_owner(c).start())
        pl.when(jnp.logical_not(away))(lambda: to_self(c).start())

    def per_chunk(c, carry):
        pl.when(c < own_chunks)(lambda: own_weight(c).wait())

        @pl.when(c >= own_chunks)
        def _():
            for p in range(PIECES):
                weight(c - own_chunks, p).wait_recv()

        send1[c] = product(1 - a, c).astype(send1.dtype)
        to_core(c).start()
        acc[c] = product(a, c)
        pl.when(c >= 1)(lambda: merge(c - 1))
        pl.when(c >= 3)(lambda: second(c - 3))
        return carry

    def merge(c):
        to_core(c).wait_recv()
        total = acc[c] + recv1[c].astype(jnp.float32)
        acc[c] = total
        send2[c] = total.astype(send2.dtype)
        for k in range(1, halves):
            to_half(c, k).start()

    lax.fori_loop(0, chunks, per_chunk, 0)
    merge(chunks - 1)
    for c in range(max(0, chunks - 3), chunks):
        second(c)

    pl.when(right)(lambda: hop(2).wait_send())
    pl.when(two & right)(lambda: hop(4).wait_send())
    pl.when(v == 0)(lambda: sideways(0).wait_send())
    pl.when(two)(lambda: sideways(2).wait_send())
    pl.when(four & (v == 1))(lambda: sideways(4).wait_send())
    for d in range(1, REACH + 1):
        pl.when(s >= d)(lambda d=d: swap(d).wait_send())
    for c in range(own_chunks):
        for p in range(PIECES):
            weight(c, p).wait_send()
    for d in range(1, lanes):
        for way in range(2):
            @pl.when(holds(way, d - 1) & may_send(way))
            def _():
                over_groups(0, lambda j: relay(way, d, j).wait_send())

    def finish(c, carry):
        to_core(c).wait_send()
        for k in range(1, halves):
            to_half(c, k).wait_send()

        @pl.when(away)
        def _():
            to_owner(c).wait_send()
            to_owner(c).wait_recv()

        pl.when(jnp.logical_not(away))(lambda: to_self(c).wait())
        return carry

    lax.fori_loop(0, chunks, finish, 0)


def on_device(queries, keys, values, lengths, output_projection_weight):
    tokens = queries.shape[0]
    cores, halves = lax.axis_size("grp"), lax.axis_size("kv")
    lanes = cores * halves
    pairs = lax.axis_size("srv") // lanes
    assert cores == 2 and pairs == 2
    q = queries.reshape(tokens, -1)
    inner = q.shape[1]
    kv = jnp.stack([keys.reshape(tokens, -1), values.reshape(tokens, -1)])
    weight = output_projection_weight.reshape(inner, -1)
    columns = weight.shape[1]
    chunk = max(128, columns // 4)
    own_chunks = columns // chunk
    chunks = own_chunks * pairs
    groups, head = keys.shape[1], keys.shape[2]
    rows = halves * tokens
    dma = pltpu.SemaphoreType.DMA
    bf16, f32 = jnp.bfloat16, jnp.float32
    vmem = pl.BlockSpec(memory_space=pltpu.VMEM)
    return pl.pallas_call(
        functools.partial(layer, (head, halves, lanes, pairs, chunk, own_chunks)),
        out_shape=jax.ShapeDtypeStruct((tokens, pairs * columns), bf16),
        in_specs=[
            pl.BlockSpec(memory_space=pltpu.SMEM), vmem, vmem,
            pl.BlockSpec(memory_space=pl.ANY),
        ],
        out_specs=pl.BlockSpec(memory_space=pl.ANY),
        scratch_shapes=[
            pltpu.VMEM((2, REACH + 1, tokens, kv.shape[2]), bf16),
            pltpu.VMEM((tokens, (REACH + 1) * tokens), f32),
            pltpu.VMEM((lanes, tokens, inner), bf16),
            pltpu.VMEM((chunks, inner, chunk), bf16),
            pltpu.VMEM((chunks, rows, chunk), bf16),
            pltpu.VMEM((chunks, rows, chunk), bf16),
            pltpu.VMEM((chunks, rows, chunk), f32),
            pltpu.VMEM((chunks, rows, chunk), bf16),
            pltpu.VMEM((chunks, halves - 1, tokens, chunk), bf16),
            pltpu.VMEM((chunks, tokens, chunk), bf16),
            dma((2,)), dma((2,)), dma((3,)), dma((2,)), dma((REACH,)), dma((REACH,)),
            dma((own_chunks,)), dma((own_chunks, PIECES)), dma((own_chunks, PIECES)),
            dma((2, lanes - 1, groups)), dma((2, lanes - 1, groups)),
            dma((chunks,)), dma((chunks,)),
            dma((chunks, halves - 1)), dma((chunks, halves - 1)),
            dma((chunks,)), dma((chunks,)),
        ],
        compiler_params=pltpu.CompilerParams(
            collective_id=0, has_side_effects=True, vmem_limit_bytes=60 * 1024 * 1024
        ),
    )(lengths, q, kv, weight)


def solution(mesh):
    placed = (
        P("srv", "kv", "grp"),
        P("srv", "kv", None),
        P("srv", "kv", None),
        P(),
        P("kv", "grp", "srv"),
    )
    return jax.shard_map(
        on_device, mesh=mesh, in_specs=placed, out_specs=P("srv", ("grp", "kv")), check_vma=False
    )
```
